32 devices in a mesh: ctx: 8 (over y, x, core), wa: 4 (over z).
Axes of the slice: x: 2, y: 2, z: 4, core: 2. Of those that a mesh axis runs over, the one named last changes fastest.
Arguments:
- block_input: bfloat16 [1024, 1088], P('ctx'), may hold values from -6 to 6
- span_table: int32 [8, 2], replicated, may hold values from 0 to 15, as said below
- doc_ids: int32 [1024], replicated, may hold values from 0 to 3, never falling along the last dimension, each value on 1 to 512 neighbouring positions
- attn_gain: float32 [1088], replicated, may hold values from 0.5 to 1.5
- attn_shift: float32 [1088], replicated, may hold values from -1.75 to 1.75
- qkv_weight: bfloat16 [1088, 3264], P('wa'), may hold values from -0.1875 to 0.1875
- query_bias: float32 [1088], replicated, may hold values from -3 to 3
- value_bias: float32 [1088], replicated, may hold values from -3 to 3
- out_weight: bfloat16 [1088, 1088], P(None, 'wa'), may hold values from -1 to 1
- out_bias: float32 [1088], replicated, may hold values from -3 to 3
- mlp_gain: float32 [1088], replicated, may hold values from 0.1 to 1.9
- mlp_shift: float32 [1088], replicated, may hold values from -1.75 to 1.75
- up_weight: bfloat16 [1088, 4352], P(None, 'wa'), may hold values from -0.1875 to 0.1875
- up_bias: float32 [4352], P('wa'), may hold values from -3 to 3
- down_weight: bfloat16 [4352, 1088], P('wa'), may hold values from -0.09375 to 0.09375
- down_bias: float32 [1088], replicated, may hold values from -6 to 6
- cotangent: bfloat16 [1024, 1088], P('ctx'), may hold values from -6 to 6
Outputs:
- block_output: bfloat16 [1024, 1088], P('ctx', 'wa')
- input_grad: bfloat16 [1024, 1088], P('ctx')
- qkv_grad: float32 [1088, 3264], P('wa', 'ctx')
- query_bias_grad: float32 [1088], replicated
- value_bias_grad: float32 [1088], replicated
- out_grad: float32 [1088, 1088], P('ctx', 'wa')
- out_bias_grad: float32 [1088], replicated
- up_grad: float32 [1088, 4352], P('ctx', 'wa')
- up_bias_grad: float32 [4352], P('wa')
- down_grad: float32 [4352, 1088], P('wa', 'ctx')
- down_bias_grad: float32 [1088], replicated
- attn_gain_grad: float32 [1088], replicated
- attn_shift_grad: float32 [1088], replicated
- mlp_gain_grad: float32 [1088], replicated
- mlp_shift_grad: float32 [1088], replicated
The draws below stay inside these ranges and needn't reach their ends.
Inputs may be any that keep to these rules, and one draw needn't show every extreme that they name: The spans of 64 tokens are numbered in sequence order; the two spans of each row of span_table have numbers that add up to the count of spans minus one, and every span stands in exactly one row. `doc_ids`: document numbers never fall along the sequence; each document holds at most 512 tokens.
All inputs are finite; a program needn't handle non-finite values.
Results may differ from the reference program's by a relative error of at most 0.033.
Values may be sent and summed in bfloat16 or wider, within the bound.
No kernel may reach another device: no remote copies, remote signals or barrier semaphores. Data moves between devices by JAX's collectives and lax.ppermute only.
A program may use at most 320 MiB of HBM per device.

```python
import math
import jax
import jax.numpy as jnp
import numpy as np
from jax import lax

D = 1088
HEADS = 17
HEAD_DIM = 64
FF = 4352
TOK_CTX = 128
TOKENS = 1024
SPAN = 64
DOCS = 4
DOC_MOST = 512


def draw_span_table(key, part):
    pair_count = TOKENS // (2 * SPAN)
    group_count = pair_count // 2
    groups = jax.random.permutation(jax.random.fold_in(key, 11), group_count).astype(jnp.int32)
    group_flips = jax.random.randint(jax.random.fold_in(key, 12), (group_count,), 0, 2, dtype=jnp.int32)
    owner = jnp.arange(pair_count, dtype=jnp.int32)
    member = owner % group_count
    upper = owner // group_count
    order = (2 * groups[member] + upper).astype(jnp.int32)
    flips = group_flips[member]
    mirror = 2 * pair_count - 1 - order
    leading = jnp.where(flips == 1, mirror, order)
    trailing = jnp.where(flips == 1, order, mirror)
    return jnp.stack([leading, trailing], axis=1).astype(jnp.int32)


def strengthened(drawn, rng, source, target, parts, factor):
    owner, partner = [(jnp.arange(drawn.shape[position]) // (drawn.shape[position] // parts)).reshape([-1 if axis == position else 1 for axis in range(drawn.ndim)]) for position in (source, target)]
    chosen = jax.random.permutation(rng, parts)[partner]
    strong = (owner == chosen) | (owner == (partner + parts // 2) % parts)
    return jnp.where(strong, factor * drawn, drawn)


def shard_levels(key, shape, split, smallest, high):
    def one(position, parts):
        draws = jax.random.uniform(jax.random.fold_in(jax.random.fold_in(key, 6), position), (parts,), jnp.float32, smallest / len(split), high / len(split))
        return jnp.repeat(jnp.exp(draws), shape[position] // parts).reshape((-1,) + (1,) * (len(shape) - position - 1))

    factor_of = one(*split[0])
    for cut in split[1:]:
        factor_of = factor_of * one(*cut)
    return factor_of


def split_up(count, total, bound, skew):
    portions = [(1 << 20) // math.isqrt(standing ** skew) + 1 for standing in range(2, count + 1)]
    surplus, counts = total - bound - (count - 1), [1] * (count - 1)
    while surplus > 0:
        movable = [i for i in range(count - 1) if counts[i] < bound]
        whole, remaining = sum([portions[i] for i in movable]), surplus
        for i in movable:
            addition = min(bound - counts[i], max(1, remaining * portions[i] // whole), surplus)
            counts[i] = counts[i] + addition
            surplus = surplus - addition
    return np.array([bound] + counts)


def ragged(own_key, number_of, total, bound, lean):
    if number_of == 2:
        one = jax.random.randint(own_key, (), max(1, total - bound), min(bound, total - 1) + 1)
        return jnp.stack([one, total - one])
    tallies = jnp.asarray(split_up(number_of, total, bound, lean), jnp.int32)
    twos = (number_of - 1) // 2
    source_of, sink = tallies[1:1 + 2 * twos:2], tallies[2:2 + 2 * twos:2]
    slack = jnp.minimum(source_of - 1, bound - sink)
    passed = jax.random.randint(jax.random.fold_in(own_key, 1), (twos,), 0, 1 << 20) % (slack + 1)
    tallies = tallies.at[1:1 + 2 * twos:2].set(source_of - passed).at[2:2 + 2 * twos:2].set(sink + passed)
    return tallies[jax.random.permutation(jax.random.fold_in(own_key, 2), number_of)]


def scatter_about(key, extent, spread, limit, cuts=(), kind=jnp.bfloat16):
    drawn = spread * jax.random.normal(key, extent, jnp.float32)
    if cuts:
        drawn = drawn * shard_levels(key, extent, cuts, -0.22, 0.18)
    return jnp.clip(drawn, -limit, limit).astype(kind)


def gaussian_with(own_key, dims, width, most, cuts, heavy, held_as=jnp.bfloat16):
    drawn = width * jax.random.normal(own_key, dims, jnp.float32)
    if cuts:
        drawn = drawn * shard_levels(own_key, dims, cuts, -0.22, 0.18)
    return jnp.clip(strengthened(drawn, jax.random.fold_in(own_key, 3), *heavy), -most, most).astype(held_as)


def setup_inputs(seed: int = 0) -> dict:
    streams_of = jax.random.split(jax.random.key(seed), 18)
    return {
        "block_input": scatter_about(streams_of[0], (TOKENS, D), 1.0, 6.0, ((0, 8),)),
        "span_table": draw_span_table(jax.random.fold_in(streams_of[17], 71), 0),
        "doc_ids": jnp.searchsorted(jnp.cumsum(ragged(streams_of[2], DOCS, TOKENS, DOC_MOST, 1)), jnp.arange(TOKENS), side="right").astype(jnp.int32),
        "attn_gain": jnp.clip(1.0 + 0.1 * jax.random.normal(streams_of[3], (D,), jnp.float32), 0.5, 1.5),
        "attn_shift": scatter_about(streams_of[4], (D,), 0.3, 1.75, (), jnp.float32),
        "qkv_weight": scatter_about(streams_of[5], (D, 3 * D), D ** -0.5, 0.1875, ((0, 4),)),
        "query_bias": scatter_about(streams_of[6], (D,), 0.5, 3.0, (), jnp.float32),
        "value_bias": scatter_about(streams_of[7], (D,), 0.5, 3.0, (), jnp.float32),
        "out_weight": scatter_about(streams_of[8], (D, D), (max(2, 16 * D // DOC_MOST)) ** -0.5, 1.0, ((1, 4),)),
        "out_bias": scatter_about(streams_of[9], (D,), 0.5, 3.0, (), jnp.float32),
        "mlp_gain": jnp.clip(1.0 + 0.18 * jax.random.normal(streams_of[10], (D,), jnp.float32), 0.1, 1.9),
        "mlp_shift": scatter_about(streams_of[11], (D,), 0.3, 1.75, (), jnp.float32),
        "up_weight": scatter_about(streams_of[12], (D, FF), D ** -0.5, 0.1875, ((1, 4),)),
        "up_bias": scatter_about(streams_of[13], (FF,), 0.5, 3.0, ((0, 4),), jnp.float32),
        "down_weight": scatter_about(streams_of[14], (FF, D), FF ** -0.5, 0.09375, ((0, 4),)),
        "down_bias": scatter_about(streams_of[15], (D,), 1.0, 6.0, (), jnp.float32),
        "cotangent": gaussian_with(streams_of[16], (TOKENS, D), 1.0, 6.0, ((0, 8),), (0, 1, 8, 2.0)),
    }


norm_eps = 1e-05
root_half = 0.7071067811865476
inv_root_tau = 0.3989422804014327

def rounded(value):
    return lax.optimization_barrier(value.astype(jnp.bfloat16))

def gelu_value(pre):
    return 0.5 * pre * (1.0 + lax.erf(pre * root_half))

def gelu_slope(pre):
    return 0.5 * (1.0 + lax.erf(pre * root_half)) + pre * inv_root_tau * jnp.exp(-0.5 * pre * pre)

def norm_parts(values, gain, shift):
    center = lax.optimization_barrier(jnp.mean(values, axis=-1, keepdims=True))
    square = lax.optimization_barrier(jnp.mean(values * values, axis=-1, keepdims=True))
    inv_std = lax.rsqrt(square - center * center + norm_eps)
    normed = (values - center) * inv_std
    return (normed, inv_std, normed * gain + shift)

def norm_back(grad_out, normed, inv_std, gain):
    scaled = grad_out * gain
    return inv_std * (scaled - lax.optimization_barrier(jnp.mean(scaled, axis=-1, keepdims=True)) - normed * lax.optimization_barrier(jnp.mean(scaled * normed, axis=-1, keepdims=True)))

def token_places(row_ids, span_table, doc_ids):
    owner = row_ids // TOK_CTX
    halves = row_ids % TOK_CTX // SPAN
    places = (span_table[owner, halves] * SPAN + row_ids % SPAN).astype(jnp.int32)
    return (places, doc_ids[places])

def reference(block_input, span_table, doc_ids, attn_gain, attn_shift, qkv_weight, query_bias, value_bias, out_weight, out_bias, mlp_gain, mlp_shift, up_weight, up_bias, down_weight, down_bias, cotangent):
    score_scale = float(HEAD_DIM) ** (-0.5)
    row_ids = jnp.arange(TOKENS, dtype=jnp.int32)
    places, docs = token_places(row_ids, span_table, doc_ids)
    input_f = block_input.astype(jnp.float32)
    attn_hat, attn_inv, attn_norm = norm_parts(input_f, attn_gain, attn_shift)
    normed_in = attn_norm.astype(jnp.bfloat16)
    bias_row = jnp.concatenate([query_bias, jnp.zeros_like(query_bias), value_bias])
    qkv_all = rounded(jnp.dot(normed_in, qkv_weight, preferred_element_type=jnp.float32) + bias_row)
    qkv_f = qkv_all.astype(jnp.float32)
    query_heads = qkv_f[:, :D].reshape(TOKENS, HEADS, HEAD_DIM)
    key_heads = qkv_f[:, D:2 * D].reshape(TOKENS, HEADS, HEAD_DIM)
    val_heads = qkv_f[:, 2 * D:].reshape(TOKENS, HEADS, HEAD_DIM)
    block_rows = math.gcd(TOKENS, 512)
    block_count = TOKENS // block_rows

    def split_rows(values):
        return values.reshape((block_count, block_rows) + values.shape[1:])

    def visible(place_block, doc_block):
        return (docs[None, :] == doc_block[:, None]) & (places[None, :] <= place_block[:, None])

    def forward_block(inputs):
        query_block, place_block, doc_block = inputs
        allowed = visible(place_block, doc_block)
        scores = jnp.einsum('qhd,khd->hqk', query_block, key_heads) * score_scale
        scores = jnp.where(allowed[None], scores, -jnp.inf)
        row_top = lax.optimization_barrier(jnp.max(scores, axis=-1, keepdims=True))
        log_block = row_top[..., 0] + jnp.log(lax.optimization_barrier(jnp.sum(jnp.exp(scores - row_top), axis=-1)))
        weights = rounded(jnp.exp(scores - log_block[..., None])).astype(jnp.float32)
        mixed = jnp.einsum('hqk,khd->qhd', weights, val_heads)
        return (mixed, log_block.T)
    mixed_all, log_all = lax.map(forward_block, (split_rows(query_heads), split_rows(places), split_rows(docs)))
    attn_out = rounded(mixed_all.reshape(TOKENS, D))
    log_norm = log_all.reshape(TOKENS, HEADS)
    resid = input_f + jnp.dot(attn_out, out_weight, preferred_element_type=jnp.float32) + out_bias
    mlp_hat, mlp_inv, mlp_norm = norm_parts(resid, mlp_gain, mlp_shift)
    normed_mid = mlp_norm.astype(jnp.bfloat16)
    hidden_pre = jnp.dot(normed_mid, up_weight, preferred_element_type=jnp.float32) + up_bias
    hidden_act = gelu_value(hidden_pre).astype(jnp.bfloat16)
    block_output = (resid + jnp.dot(hidden_act, down_weight, preferred_element_type=jnp.float32) + down_bias).astype(jnp.bfloat16)
    grad_f = cotangent.astype(jnp.float32)
    down_bias_grad = lax.optimization_barrier(jnp.sum(grad_f, axis=0))
    down_grad = jnp.dot(hidden_act.T, cotangent, preferred_element_type=jnp.float32)
    hidden_grad = jnp.dot(cotangent, down_weight.T, preferred_element_type=jnp.float32) * gelu_slope(hidden_pre)
    up_bias_grad = lax.optimization_barrier(jnp.sum(hidden_grad, axis=0))
    hidden_grad_b = hidden_grad.astype(jnp.bfloat16)
    up_grad = jnp.dot(normed_mid.T, hidden_grad_b, preferred_element_type=jnp.float32)
    mid_grad = jnp.dot(hidden_grad_b, up_weight.T, preferred_element_type=jnp.float32)
    mlp_gain_grad = lax.optimization_barrier(jnp.sum(mid_grad * mlp_hat, axis=0))
    mlp_shift_grad = lax.optimization_barrier(jnp.sum(mid_grad, axis=0))
    resid_grad = grad_f + norm_back(mid_grad, mlp_hat, mlp_inv, mlp_gain)
    out_bias_grad = lax.optimization_barrier(jnp.sum(resid_grad, axis=0))
    resid_grad_b = resid_grad.astype(jnp.bfloat16)
    out_grad = jnp.dot(attn_out.T, resid_grad_b, preferred_element_type=jnp.float32)
    attn_grad = rounded(jnp.dot(resid_grad_b, out_weight.T, preferred_element_type=jnp.float32))
    grad_heads = attn_grad.astype(jnp.float32).reshape(TOKENS, HEADS, HEAD_DIM)
    out_heads = attn_out.astype(jnp.float32).reshape(TOKENS, HEADS, HEAD_DIM)
    delta = lax.optimization_barrier(jnp.sum(grad_heads * out_heads, axis=-1))
    log_hi = rounded(log_norm)
    log_lo = rounded(log_norm - log_hi.astype(jnp.float32))
    log_sent = log_hi.astype(jnp.float32) + log_lo.astype(jnp.float32)
    delta_hi = rounded(delta)
    delta_lo = rounded(delta - delta_hi.astype(jnp.float32))
    delta_sent = delta_hi.astype(jnp.float32) + delta_lo.astype(jnp.float32)

    def backward_block(grads, inputs):
        key_acc, val_acc = grads
        query_block, grad_block, log_block, delta_block, place_block, doc_block = inputs
        allowed = visible(place_block, doc_block)
        scores = jnp.einsum('qhd,khd->hqk', query_block, key_heads) * score_scale
        exp_scores = jnp.exp(jnp.where(allowed[None], scores - log_block.T[..., None], -jnp.inf))
        slopes = jnp.einsum('qhd,khd->hqk', grad_block, val_heads)
        score_grad = rounded(exp_scores * (slopes - delta_block.T[..., None])).astype(jnp.float32)
        weights = rounded(exp_scores).astype(jnp.float32)
        query_grad = jnp.einsum('hqk,khd->qhd', score_grad, key_heads) * score_scale
        key_acc = key_acc + jnp.einsum('hqk,qhd->khd', score_grad, query_block)
        val_acc = val_acc + jnp.einsum('hqk,qhd->khd', weights, grad_block)
        return ((key_acc, val_acc), query_grad)
    zero_heads = jnp.zeros((TOKENS, HEADS, HEAD_DIM), jnp.float32)
    sums_kv, query_grads = lax.scan(backward_block, (zero_heads, zero_heads), (split_rows(query_heads), split_rows(grad_heads), split_rows(log_sent), split_rows(delta_sent), split_rows(places), split_rows(docs)))
    key_grad, val_grad = sums_kv
    qkv_grad_b = rounded(jnp.concatenate([query_grads.reshape(TOKENS, D), (key_grad * score_scale).reshape(TOKENS, D), val_grad.reshape(TOKENS, D)], axis=1))
    grad_sums = lax.optimization_barrier(jnp.sum(qkv_grad_b.astype(jnp.float32), axis=0))
    query_bias_grad = grad_sums[:D]
    value_bias_grad = grad_sums[2 * D:]
    qkv_grad = jnp.dot(normed_in.T, qkv_grad_b, preferred_element_type=jnp.float32)
    normed_grad = jnp.dot(qkv_grad_b, qkv_weight.T, preferred_element_type=jnp.float32)
    attn_gain_grad = lax.optimization_barrier(jnp.sum(normed_grad * attn_hat, axis=0))
    attn_shift_grad = lax.optimization_barrier(jnp.sum(normed_grad, axis=0))
    input_grad = (resid_grad + norm_back(normed_grad, attn_hat, attn_inv, attn_gain)).astype(jnp.bfloat16)
    return (block_output, input_grad, qkv_grad, query_bias_grad, value_bias_grad, out_grad, out_bias_grad, up_grad, up_bias_grad, down_grad, down_bias_grad, attn_gain_grad, attn_shift_grad, mlp_gain_grad, mlp_shift_grad)
```

```python
import jax
import jax.numpy as jnp
from jax import lax
from jax.sharding import PartitionSpec as P

HEADS = 17
HEAD_DIM = 64
SPAN = 64
DIRECT_MOST = 8


norm_eps = 1e-05
root_half = 0.7071067811865476
inv_root_tau = 0.3989422804014327
f32 = jnp.float32
bf16 = jnp.bfloat16


def rounded(value):
    return lax.optimization_barrier(value.astype(bf16))


def gelu_value(pre):
    return 0.5 * pre * (1.0 + lax.erf(pre * root_half))


def gelu_slope(pre):
    return 0.5 * (1.0 + lax.erf(pre * root_half)) + pre * inv_root_tau * jnp.exp(-0.5 * pre * pre)


def norm_parts(values, gain, shift):
    center = jnp.mean(values, axis=0, keepdims=True)
    square = jnp.mean(values * values, axis=0, keepdims=True)
    inv_std = lax.rsqrt(square - center * center + norm_eps)
    normed = (values - center) * inv_std
    return normed, inv_std, normed * gain[:, None] + shift[:, None]


def dot(left, right, left_dim, right_dim):
    return lax.dot_general(
        left, right, (((left_dim,), (right_dim,)), ((), ())), preferred_element_type=f32
    )


def swap(value, axis, flip):
    count = lax.axis_size(axis)
    return lax.ppermute(value, axis, [(i, i ^ flip) for i in range(count)])


def bit_order(count):
    flips = [1 << i for i in range(count.bit_length() - 1)]
    return flips[1:] + flips[:1]


def gather_direct(value, axis):
    return [value] + [swap(value, axis, flip) for flip in range(1, lax.axis_size(axis))]


def gather_doubling(value, axis):
    count = lax.axis_size(axis)
    held, order = value[None], [0]
    for flip in bit_order(count):
        held = jnp.concatenate([held, swap(held, axis, flip)], axis=0)
        order = order + [i ^ flip for i in order]
    return [held[order.index(i)] for i in range(count)]


def gather_blocks(value, axis):
    if lax.axis_size(axis) <= DIRECT_MOST:
        return gather_direct(value, axis)
    return gather_doubling(value, axis)


def exchange_direct(block_for, axis):
    me = lax.axis_index(axis)
    return [block_for(me)] + [
        swap(block_for(me ^ flip), axis, flip) for flip in range(1, lax.axis_size(axis))
    ]


def scatter_halving(blocks, axis):
    count = lax.axis_size(axis)
    held = {i: blocks[i] for i in range(count)}
    for flip in [1 << i for i in range(count.bit_length() - 1)]:
        keep = [i for i in held if not i & flip]
        sent = jnp.stack([held[i | flip] for i in keep]).astype(bf16)
        got = swap(sent, axis, flip)
        held = {i: held[i] + got[n].astype(f32) for n, i in enumerate(keep)}
    return held[0]


def sum_doubling(value, axis):
    for flip in bit_order(lax.axis_size(axis)):
        value = value + swap(value, axis, flip)
    return value


def split_pair(value):
    high = lax.reduce_precision(value, 8, 7)
    low = lax.reduce_precision(value - high, 8, 7)
    return jnp.concatenate([high, low], axis=0)


def pad_rows(value, multiple=16):
    return jnp.pad(value, ((0, -value.shape[0] % multiple), (0, 0)))


def body(
    block_input,
    span_table,
    doc_ids,
    attn_gain,
    attn_shift,
    qkv_weight,
    query_bias,
    value_bias,
    out_weight,
    out_bias,
    mlp_gain,
    mlp_shift,
    up_weight,
    up_bias,
    down_weight,
    down_bias,
    cotangent,
):
    tok, width = block_input.shape
    wa_count, ctx_count = lax.axis_size("wa"), lax.axis_size("ctx")
    wa, ctx = lax.axis_index("wa"), lax.axis_index("ctx")
    cols = width // wa_count
    slots = -(-HEADS // wa_count)
    group = slots * HEAD_DIM
    scale = float(HEAD_DIM) ** (-0.5)

    def my_cols(value):
        return lax.dynamic_slice_in_dim(value, wa * cols, cols, 0)

    def group_row(member):
        return jnp.minimum(member * slots, HEADS - slots) * HEAD_DIM

    def place_groups(pieces, axis):
        stacked = jnp.stack(pieces)
        ordered = [
            lax.dynamic_index_in_dim(stacked, wa ^ i, 0, keepdims=False) for i in range(wa_count)
        ]
        spare = (wa_count * slots - HEADS) * HEAD_DIM
        ordered[-1] = lax.slice_in_dim(ordered[-1], spare, group, axis=axis)
        return jnp.concatenate(ordered, axis=axis)

    def place_cols(pieces):
        full = jnp.zeros((wa_count * pieces[0].shape[0],) + pieces[0].shape[1:], pieces[0].dtype)
        for i, piece in enumerate(pieces):
            full = lax.dynamic_update_slice_in_dim(full, piece, (wa ^ i) * piece.shape[0], 0)
        return full

    input_t = block_input.astype(f32).T
    cot_t = cotangent.T
    attn_hat, attn_inv, attn_norm = norm_parts(input_t, attn_gain, attn_shift)
    normed_in = attn_norm.astype(bf16)
    normed_cols = my_cols(normed_in)
    qkv_part = dot(qkv_weight, normed_cols, 0, 0).reshape(3, width, tok)

    def group_rows(value, member):
        return lax.dynamic_slice_in_dim(value, group_row(member), group, 1)

    qkv_sent = qkv_part.astype(bf16)
    qkv_got = exchange_direct(lambda member: group_rows(qkv_sent, member), "wa")
    bias_rows = jnp.stack([query_bias, jnp.zeros_like(query_bias), value_bias])
    qkv_sum = group_rows(qkv_part, wa) + group_rows(bias_rows, wa)[:, :, None]
    for piece in qkv_got[1:]:
        qkv_sum = qkv_sum + piece.astype(f32)
    qkv_own = rounded(qkv_sum)
    own_q = qkv_own[0].reshape(slots, HEAD_DIM, tok)
    own_k = qkv_own[1].reshape(slots, HEAD_DIM, tok)
    own_v = qkv_own[2].reshape(slots, HEAD_DIM, tok)

    sources = ctx ^ jnp.arange(ctx_count, dtype=jnp.int32)
    holder = sources[:, None, None] == jnp.arange(ctx_count, dtype=jnp.int32)[None, :, None]
    spans = jnp.sum(jnp.where(holder, span_table[None], 0), axis=1)
    all_place = (spans[:, :, None] * SPAN + jnp.arange(SPAN, dtype=jnp.int32)).reshape(-1)
    span_docs = doc_ids.reshape(-1, SPAN)
    span_is = spans.reshape(-1)[:, None, None] == jnp.arange(span_docs.shape[0])[None, :, None]
    all_doc = jnp.sum(jnp.where(span_is, span_docs[None], 0), axis=1).reshape(-1)
    own_place, own_doc = all_place[:tok], all_doc[:tok]

    kv_blocks = gather_blocks(qkv_own[1:].reshape(2 * group, tok), "ctx")
    kv_all = jnp.concatenate(kv_blocks, axis=1).reshape(2, slots, HEAD_DIM, ctx_count * tok)
    all_k, all_v = kv_all[0], kv_all[1]
    allowed = (all_doc[:, None] == own_doc[None, :]) & (all_place[:, None] <= own_place[None, :])

    def heads_dot(spec, left, right):
        return jnp.einsum(spec, left, right, preferred_element_type=f32)

    scores = heads_dot("hdk,hdq->hkq", all_k, own_q) * scale
    masked = jnp.where(allowed[None], scores, -jnp.inf)
    top = jnp.max(masked, axis=1, keepdims=True)
    exp_scores = jnp.exp(masked - top)
    total = jnp.sum(exp_scores, axis=1, keepdims=True)
    attn_out = rounded(heads_dot("hdk,hkq->hdq", all_v, exp_scores.astype(bf16)) / total)
    log_norm = (top + jnp.log(total))[:, 0]

    early, _ = lax.optimization_barrier(
        (jnp.concatenate([cot_t, normed_cols, qkv_own[0]], axis=0), kv_blocks)
    )
    early_all = jnp.concatenate(gather_doubling(early, "ctx"), axis=1)
    cot_all = early_all[:width]
    normed_cols_all = early_all[width : width + cols]
    all_q = early_all[width + cols :].reshape(slots, HEAD_DIM, ctx_count * tok)

    attn_full = place_groups(gather_direct(attn_out.reshape(group, tok), "wa"), 0)
    resid_cols = my_cols(input_t) + dot(out_weight, attn_full, 0, 0) + my_cols(out_bias)[:, None]
    resid = place_cols(gather_direct(resid_cols.astype(bf16), "wa")).astype(f32)
    mlp_hat, mlp_inv, mlp_norm = norm_parts(resid, mlp_gain, mlp_shift)
    normed_mid = rounded(mlp_norm)

    grad_pre = dot(down_weight, cotangent, 1, 1)
    hidden_pre = dot(up_weight, normed_mid, 0, 0) + up_bias[:, None]
    hidden_act = gelu_value(hidden_pre).astype(bf16)
    hidden_grad = grad_pre * gelu_slope(hidden_pre)
    up_bias_part = jnp.sum(hidden_grad, axis=1)
    mid_part = lax.optimization_barrier(dot(up_weight, rounded(hidden_grad), 1, 0))
    scaled_part = mid_part * mlp_gain[:, None]
    sums_part = jnp.stack(
        [jnp.sum(scaled_part, axis=0), jnp.sum(scaled_part * mlp_hat, axis=0)]
    )
    sums_sent = pad_rows(split_pair(sums_part)).astype(bf16)
    mid_sent = mid_part.astype(bf16)

    def mid_block(member):
        rows = lax.dynamic_slice_in_dim(mid_sent, member * cols, cols, 0)
        return jnp.concatenate([rows, sums_sent], axis=0)

    mid_sum = sum(piece.astype(f32) for piece in exchange_direct(mid_block, "wa"))
    mid_cols = mid_sum[:cols]
    row_sums = (mid_sum[cols : cols + 2] + mid_sum[cols + 2 : cols + 4]) / width
    hat_cols = my_cols(mlp_hat)
    resid_grad = my_cols(cot_t).astype(f32) + mlp_inv * (
        mid_cols * my_cols(mlp_gain)[:, None] - row_sums[:1] - hat_cols * row_sums[1:]
    )
    resid_grad_b = rounded(resid_grad)

    attn_part = dot(out_weight, resid_grad_b, 1, 0)
    attn_sent = attn_part.astype(bf16)
    attn_got = exchange_direct(
        lambda member: lax.dynamic_slice_in_dim(attn_sent, group_row(member), group, 0), "wa"
    )
    attn_sum = lax.dynamic_slice_in_dim(attn_part, group_row(wa), group, 0)
    for piece in attn_got[1:]:
        attn_sum = attn_sum + piece.astype(f32)
    attn_grad = rounded(attn_sum)
    own_g = attn_grad.reshape(slots, HEAD_DIM, tok)
    delta = jnp.sum(own_g.astype(f32) * attn_out.astype(f32), axis=1)
    own_pairs = split_pair(jnp.concatenate([log_norm, delta], axis=0))
    late = jnp.concatenate([attn_grad, pad_rows(own_pairs).astype(bf16)], axis=0)
    late_all = jnp.concatenate(gather_blocks(late, "ctx"), axis=1)
    all_g = late_all[:group].reshape(slots, HEAD_DIM, ctx_count * tok)
    stats = late_all[group : group + 2 * slots].astype(f32) + late_all[
        group + 2 * slots : group + 4 * slots
    ].astype(f32)
    all_log, all_delta = stats[:slots, None], stats[slots:, None]
    own_stats = own_pairs[: 2 * slots] + own_pairs[2 * slots :]
    own_log, own_delta = own_stats[:slots, None], own_stats[slots:, None]

    back = jnp.exp(jnp.where(allowed[None], scores - own_log, -jnp.inf))
    slopes = heads_dot("hdk,hdq->hkq", all_v, own_g)
    score_grad = (back * (slopes - own_delta)).astype(bf16)
    query_grad = heads_dot("hdk,hkq->hdq", all_k, score_grad) * scale

    seen = (own_doc[:, None] == all_doc[None, :]) & (own_place[:, None] <= all_place[None, :])
    scores_k = heads_dot("hdk,hdq->hkq", own_k, all_q) * scale
    back_k = jnp.exp(jnp.where(seen[None], scores_k - all_log, -jnp.inf))
    slopes_k = heads_dot("hdk,hdq->hkq", own_v, all_g)
    score_grad_k = (back_k * (slopes_k - all_delta)).astype(bf16)
    key_grad = heads_dot("hdq,hkq->hdk", all_q, score_grad_k) * scale
    val_grad = heads_dot("hdq,hkq->hdk", all_g, back_k.astype(bf16))
    qkv_grad_own = rounded(jnp.stack([query_grad, key_grad, val_grad])).reshape(3, group, tok)

    qkv_grad_full = place_groups(gather_direct(qkv_grad_own, "wa"), 1).reshape(3 * width, tok)
    normed_grad = place_cols(
        gather_direct(dot(qkv_weight, qkv_grad_full, 1, 0).astype(bf16), "wa")
    ).astype(f32)

    down_part = dot(down_weight, hidden_act, 0, 0)
    down_sent = down_part.astype(bf16)
    down_cols = my_cols(down_part) + sum(
        piece.astype(f32)
        for piece in exchange_direct(
            lambda member: lax.dynamic_slice_in_dim(down_sent, member * cols, cols, 0), "wa"
        )[1:]
    )
    block_output = (resid_cols + down_cols + my_cols(down_bias)[:, None]).astype(bf16).T

    col_sums = jnp.stack(
        [
            jnp.sum(mid_cols * hat_cols, axis=1),
            jnp.sum(mid_cols, axis=1),
            jnp.sum(resid_grad, axis=1),
        ]
    )
    flat = split_pair(col_sums).reshape(-1)
    flat = jnp.pad(flat, (0, -flat.shape[0] % (16 * tok))).reshape(-1, tok)
    side = jnp.concatenate([resid_grad_b, flat.astype(bf16)], axis=0)
    side_all = place_cols([piece[None] for piece in gather_direct(side, "wa")])
    resid_grad_full = side_all[:, :cols].reshape(width, tok).astype(f32)
    sums_flat = side_all[:, cols:].reshape(wa_count, -1)[:, : 6 * cols].reshape(wa_count, 6, cols)
    sums_full = sums_flat[:, :3].astype(f32) + sums_flat[:, 3:].astype(f32)
    sums_full = sums_full.transpose(1, 0, 2).reshape(3, width)

    scaled = normed_grad * attn_gain[:, None]
    input_grad = resid_grad_full + attn_inv * (
        scaled
        - jnp.mean(scaled, axis=0, keepdims=True)
        - attn_hat * jnp.mean(scaled * attn_hat, axis=0, keepdims=True)
    )
    input_grad = input_grad.astype(bf16).T

    mid_all = jnp.concatenate(gather_doubling(normed_mid, "ctx"), axis=1)
    pre_all = dot(up_weight, mid_all, 0, 0) + up_bias[:, None]
    act_all = gelu_value(pre_all).astype(bf16)
    hidden_grad_all = (dot(down_weight, cot_all, 1, 0) * gelu_slope(pre_all)).astype(bf16)
    share = width // ctx_count

    def my_share(value):
        return lax.dynamic_slice_in_dim(value, ctx * share, share, 0)

    up_grad = dot(my_share(mid_all), hidden_grad_all, 1, 1)
    down_grad = dot(act_all, my_share(cot_all), 1, 1)
    out_part = dot(attn_full, resid_grad_b, 1, 1)
    out_grad = scatter_halving(
        [
            lax.dynamic_slice_in_dim(out_part, (ctx ^ i) * share, share, 0)
            for i in range(ctx_count)
        ],
        "ctx",
    )
    qkv_share = 3 * width // ctx_count
    if ctx_count <= DIRECT_MOST:
        qkv_blocks = exchange_direct(
            lambda member: lax.dynamic_slice_in_dim(
                qkv_grad_full, member * qkv_share, qkv_share, 0
            ),
            "ctx",
        )
    else:
        parted = qkv_grad_full.reshape(ctx_count, qkv_share, tok)
        parted = lax.all_to_all(parted, "ctx", 0, 0)
        qkv_blocks = [
            lax.dynamic_index_in_dim(parted, ctx ^ i, 0, keepdims=False) for i in range(ctx_count)
        ]
    qkv_grad = dot(normed_cols_all, jnp.concatenate(qkv_blocks, axis=1), 1, 1)

    qkv_sums = jnp.sum(qkv_grad_full.astype(f32), axis=1)
    packed = jnp.stack(
        [
            jnp.sum(normed_grad * attn_hat, axis=1),
            jnp.sum(normed_grad, axis=1),
            sums_full[0],
            sums_full[1],
            qkv_sums[:width],
            qkv_sums[2 * width :],
            sums_full[2],
            jnp.sum(cotangent.astype(f32), axis=0),
        ]
    )
    up_rows = up_bias_part.reshape(-1, width)
    vectors = sum_doubling(jnp.concatenate([packed, up_rows], axis=0), "ctx")
    return (
        block_output,
        input_grad,
        qkv_grad,
        vectors[4],
        vectors[5],
        out_grad,
        vectors[6],
        up_grad,
        vectors[8:].reshape(-1),
        down_grad,
        vectors[7],
        vectors[0],
        vectors[1],
        vectors[2],
        vectors[3],
    )


def solution(mesh):
    placed = (
        P("ctx", None),
        P(),
        P(),
        P(),
        P(),
        P("wa", None),
        P(),
        P(),
        P(None, "wa"),
        P(),
        P(),
        P(),
        P(None, "wa"),
        P("wa"),
        P("wa", None),
        P(),
        P("ctx", None),
    )
    return jax.shard_map(
        body,
        mesh=mesh,
        in_specs=placed,
        out_specs=(
            P("ctx", "wa"),
            P("ctx", None),
            P("wa", "ctx"),
            P(),
            P(),
            P("ctx", "wa"),
            P(),
            P("ctx", "wa"),
            P("wa"),
            P("wa", "ctx"),
            P(),
            P(),
            P(),
            P(),
            P(),
        ),
        check_vma=False,
    )
```

```python
import jax
import jax.numpy as jnp
from jax import lax
from jax.experimental import pallas as pl
from jax.experimental.pallas import tpu as pltpu
from jax.sharding import PartitionSpec as P

HEADS = 17
HEAD_DIM = 64
SPAN = 64
DIRECT_MOST = 8


norm_eps = 1e-05
root_half = 0.7071067811865476
inv_root_tau = 0.3989422804014327
f32 = jnp.float32
bf16 = jnp.bfloat16


def rounded(value):
    return lax.optimization_barrier(value.astype(bf16))


def gelu_value(pre):
    return 0.5 * pre * (1.0 + lax.erf(pre * root_half))


def gelu_slope(pre):
    return 0.5 * (1.0 + lax.erf(pre * root_half)) + pre * inv_root_tau * jnp.exp(-0.5 * pre * pre)


def norm_parts(values, gain, shift):
    center = jnp.mean(values, axis=0, keepdims=True)
    square = jnp.mean(values * values, axis=0, keepdims=True)
    inv_std = lax.rsqrt(square - center * center + norm_eps)
    normed = (values - center) * inv_std
    return normed, inv_std, normed * gain[:, None] + shift[:, None]


def dot(left, right, left_dim, right_dim):
    return lax.dot_general(
        left, right, (((left_dim,), (right_dim,)), ((), ())), preferred_element_type=f32
    )


def swap(value, axis, flip):
    count = lax.axis_size(axis)
    return lax.ppermute(value, axis, [(i, i ^ flip) for i in range(count)])


def bit_order(count):
    flips = [1 << i for i in range(count.bit_length() - 1)]
    return flips[1:] + flips[:1]


def gather_direct(value, axis):
    return [value] + [swap(value, axis, flip) for flip in range(1, lax.axis_size(axis))]


def gather_doubling(value, axis):
    count = lax.axis_size(axis)
    held, order = value[None], [0]
    for flip in bit_order(count):
        held = jnp.concatenate([held, swap(held, axis, flip)], axis=0)
        order = order + [i ^ flip for i in order]
    return [held[order.index(i)] for i in range(count)]


def gather_blocks(value, axis):
    if lax.axis_size(axis) <= DIRECT_MOST:
        return gather_direct(value, axis)
    return gather_doubling(value, axis)


def exchange_direct(block_for, axis):
    me = lax.axis_index(axis)
    return [block_for(me)] + [
        swap(block_for(me ^ flip), axis, flip) for flip in range(1, lax.axis_size(axis))
    ]


def scatter_halving(blocks, axis):
    count = lax.axis_size(axis)
    held = {i: blocks[i] for i in range(count)}
    for flip in [1 << i for i in range(count.bit_length() - 1)]:
        keep = [i for i in held if not i & flip]
        sent = jnp.stack([held[i | flip] for i in keep]).astype(bf16)
        got = swap(sent, axis, flip)
        held = {i: held[i] + got[n].astype(f32) for n, i in enumerate(keep)}
    return held[0]


def sum_doubling(value, axis, steps=None):
    flips = bit_order(lax.axis_size(axis))
    for flip in flips[steps] if steps else flips:
        value = value + swap(value, axis, flip)
    return value


def join_tokens(blocks, heights):
    count, tok = len(blocks), blocks[0].shape[1]
    starts = [sum(heights[:n]) for n in range(len(heights))]
    if count > DIRECT_MOST:
        whole = jnp.concatenate(blocks, axis=1)
        return [whole[start : start + height] for start, height in zip(starts, heights)]

    def kernel(*refs):
        for n, (start, height) in enumerate(zip(starts, heights)):
            for i in range(count):
                refs[count + n][:, i * tok : (i + 1) * tok] = refs[i][start : start + height, :]

    size = sum(heights) * count * tok
    return pl.pallas_call(
        kernel,
        out_shape=[
            jax.ShapeDtypeStruct((height, count * tok), blocks[0].dtype) for height in heights
        ],
        cost_estimate=pl.CostEstimate(flops=size, bytes_accessed=4 * size, transcendentals=0),
    )(*blocks)


def token_product(left, blocks):
    count, (height, tok) = len(blocks), blocks[0].shape
    if count > DIRECT_MOST:
        return dot(left, jnp.concatenate(blocks, axis=1), 1, 1)

    def kernel(left_ref, *refs):
        out_ref, held = refs[count], refs[count + 1]
        for i in range(count):
            held[:, i * tok : (i + 1) * tok] = refs[i][...]
        out_ref[...] = dot(left_ref[...], held[...], 1, 1)

    return pl.pallas_call(
        kernel,
        out_shape=jax.ShapeDtypeStruct((left.shape[0], height), f32),
        scratch_shapes=[pltpu.VMEM((height, count * tok), blocks[0].dtype)],
        cost_estimate=pl.CostEstimate(
            flops=2 * left.shape[0] * height * count * tok,
            bytes_accessed=4 * height * count * tok,
            transcendentals=0,
        ),
    )(left, *blocks)


def after(value, other):
    return lax.optimization_barrier((value, other))[0]


def split_pair(value):
    high = lax.reduce_precision(value, 8, 7)
    low = lax.reduce_precision(value - high, 8, 7)
    return jnp.concatenate([high, low], axis=0)


def pad_rows(value, multiple=16):
    return jnp.pad(value, ((0, -value.shape[0] % multiple), (0, 0)))


def body(
    block_input,
    span_table,
    doc_ids,
    attn_gain,
    attn_shift,
    qkv_weight,
    query_bias,
    value_bias,
    out_weight,
    out_bias,
    mlp_gain,
    mlp_shift,
    up_weight,
    up_bias,
    down_weight,
    down_bias,
    cotangent,
):
    tok, width = block_input.shape
    wa_count, ctx_count = lax.axis_size("wa"), lax.axis_size("ctx")
    wa, ctx = lax.axis_index("wa"), lax.axis_index("ctx")
    cols = width // wa_count
    slots = -(-HEADS // wa_count)
    group = slots * HEAD_DIM
    scale = float(HEAD_DIM) ** (-0.5)

    def my_cols(value):
        return lax.dynamic_slice_in_dim(value, wa * cols, cols, 0)

    def group_row(member):
        return jnp.minimum(member * slots, HEADS - slots) * HEAD_DIM

    def place_groups(pieces, axis):
        stacked = jnp.stack(pieces)
        ordered = [
            lax.dynamic_index_in_dim(stacked, wa ^ i, 0, keepdims=False) for i in range(wa_count)
        ]
        spare = (wa_count * slots - HEADS) * HEAD_DIM
        ordered[-1] = lax.slice_in_dim(ordered[-1], spare, group, axis=axis)
        return jnp.concatenate(ordered, axis=axis)

    def place_cols(pieces):
        full = jnp.zeros((wa_count * pieces[0].shape[0],) + pieces[0].shape[1:], pieces[0].dtype)
        for i, piece in enumerate(pieces):
            full = lax.dynamic_update_slice_in_dim(full, piece, (wa ^ i) * piece.shape[0], 0)
        return full

    input_t = block_input.astype(f32).T
    cot_t = cotangent.T
    attn_hat, attn_inv, attn_norm = norm_parts(input_t, attn_gain, attn_shift)
    normed_in = attn_norm.astype(bf16)
    normed_cols = my_cols(normed_in)
    qkv_part = dot(qkv_weight, normed_cols, 0, 0).reshape(3, width, tok)

    def group_rows(value, member):
        return lax.dynamic_slice_in_dim(value, group_row(member), group, 1)

    def group_sums(part, sent, bias_rows):
        got = exchange_direct(lambda member: group_rows(sent, member), "wa")
        total = group_rows(part, wa) + group_rows(bias_rows, wa)[:, :, None]
        for piece in got[1:]:
            total = total + piece.astype(f32)
        return rounded(total)

    qkv_sent = qkv_part.astype(bf16)
    cot_blocks = gather_blocks(after(cot_t, qkv_sent), "ctx")
    own_kv = group_sums(
        qkv_part[1:], qkv_sent[1:], jnp.stack([jnp.zeros_like(value_bias), value_bias])
    )
    own_q_flat = group_sums(qkv_part[:1], qkv_sent[:1], query_bias[None])[0]
    own_q = own_q_flat.reshape(slots, HEAD_DIM, tok)
    own_k = own_kv[0].reshape(slots, HEAD_DIM, tok)
    own_v = own_kv[1].reshape(slots, HEAD_DIM, tok)

    sources = ctx ^ jnp.arange(ctx_count, dtype=jnp.int32)
    holder = sources[:, None, None] == jnp.arange(ctx_count, dtype=jnp.int32)[None, :, None]
    spans = jnp.sum(jnp.where(holder, span_table[None], 0), axis=1)
    all_place = (spans[:, :, None] * SPAN + jnp.arange(SPAN, dtype=jnp.int32)).reshape(-1)
    span_docs = doc_ids.reshape(-1, SPAN)
    span_is = spans.reshape(-1)[:, None, None] == jnp.arange(span_docs.shape[0])[None, :, None]
    all_doc = jnp.sum(jnp.where(span_is, span_docs[None], 0), axis=1).reshape(-1)
    own_place, own_doc = all_place[:tok], all_doc[:tok]

    def by_head(value):
        return value.reshape(slots, HEAD_DIM, ctx_count * tok)

    kv_blocks = gather_blocks(own_kv.reshape(2 * group, tok), "ctx")
    all_k, all_v = [by_head(value) for value in join_tokens(kv_blocks, [group, group])]
    allowed = (all_doc[:, None] == own_doc[None, :]) & (all_place[:, None] <= own_place[None, :])

    def heads_dot(spec, left, right):
        return jnp.einsum(spec, left, right, preferred_element_type=f32)

    scores = heads_dot("hdk,hdq->hkq", all_k, own_q) * scale
    masked = jnp.where(allowed[None], scores, -jnp.inf)
    top = jnp.max(masked, axis=1, keepdims=True)
    exp_scores = jnp.exp(masked - top)
    total = jnp.sum(exp_scores, axis=1, keepdims=True)
    attn_out = rounded(heads_dot("hdk,hkq->hdq", all_v, exp_scores.astype(bf16)) / total)
    log_norm = (top + jnp.log(total))[:, 0]

    attn_pieces = gather_direct(attn_out.reshape(group, tok), "wa")
    attn_full = place_groups(attn_pieces, 0)
    early = after(jnp.concatenate([normed_cols, own_q_flat], axis=0), attn_pieces[1])
    early_blocks = gather_blocks(early, "ctx")
    resid_cols = my_cols(input_t) + dot(out_weight, attn_full, 0, 0) + my_cols(out_bias)[:, None]
    resid = place_cols(gather_direct(resid_cols.astype(bf16), "wa")).astype(f32)
    mlp_hat, mlp_inv, mlp_norm = norm_parts(resid, mlp_gain, mlp_shift)
    normed_mid = rounded(mlp_norm)

    grad_pre = dot(down_weight, cotangent, 1, 1)
    hidden_pre = dot(up_weight, normed_mid, 0, 0) + up_bias[:, None]
    hidden_act = gelu_value(hidden_pre).astype(bf16)
    hidden_grad = grad_pre * gelu_slope(hidden_pre)
    up_bias_part = jnp.sum(hidden_grad, axis=1)
    mid_part = lax.optimization_barrier(dot(up_weight, rounded(hidden_grad), 1, 0))
    scaled_part = mid_part * mlp_gain[:, None]
    sums_part = jnp.stack(
        [jnp.sum(scaled_part, axis=0), jnp.sum(scaled_part * mlp_hat, axis=0)]
    )
    sums_sent = pad_rows(split_pair(sums_part)).astype(bf16)
    mid_sent = mid_part.astype(bf16)

    def mid_block(member):
        rows = lax.dynamic_slice_in_dim(mid_sent, member * cols, cols, 0)
        return jnp.concatenate([rows, sums_sent], axis=0)

    mid_pieces = exchange_direct(mid_block, "wa")
    mid_blocks = gather_blocks(after(normed_mid, mid_pieces[1]), "ctx")
    mid_sum = sum(piece.astype(f32) for piece in mid_pieces)
    mid_cols = mid_sum[:cols]
    row_sums = (mid_sum[cols : cols + 2] + mid_sum[cols + 2 : cols + 4]) / width
    hat_cols = my_cols(mlp_hat)
    resid_grad = my_cols(cot_t).astype(f32) + mlp_inv * (
        mid_cols * my_cols(mlp_gain)[:, None] - row_sums[:1] - hat_cols * row_sums[1:]
    )
    resid_grad_b = rounded(resid_grad)

    attn_part = dot(out_weight, resid_grad_b, 1, 0)
    attn_sent = attn_part.astype(bf16)
    attn_got = exchange_direct(
        lambda member: lax.dynamic_slice_in_dim(attn_sent, group_row(member), group, 0), "wa"
    )
    attn_sum = lax.dynamic_slice_in_dim(attn_part, group_row(wa), group, 0)
    for piece in attn_got[1:]:
        attn_sum = attn_sum + piece.astype(f32)
    attn_grad = rounded(attn_sum)
    own_g = attn_grad.reshape(slots, HEAD_DIM, tok)
    delta = jnp.sum(own_g.astype(f32) * attn_out.astype(f32), axis=1)
    own_pairs = split_pair(jnp.concatenate([log_norm, delta], axis=0))
    late = jnp.concatenate([attn_grad, pad_rows(own_pairs).astype(bf16)], axis=0)
    late_blocks = gather_blocks(late, "ctx")
    all_g, pairs = join_tokens(late_blocks, [group, late.shape[0] - group])
    all_g = by_head(all_g)
    normed_cols_all, all_q = join_tokens(early_blocks, [cols, group])
    all_q = by_head(all_q)
    pairs = pairs.astype(f32)
    stats = pairs[: 2 * slots] + pairs[2 * slots : 4 * slots]
    all_log, all_delta = stats[:slots, None], stats[slots:, None]
    own_stats = own_pairs[: 2 * slots] + own_pairs[2 * slots :]
    own_log, own_delta = own_stats[:slots, None], own_stats[slots:, None]

    back = jnp.exp(jnp.where(allowed[None], scores - own_log, -jnp.inf))
    slopes = heads_dot("hdk,hdq->hkq", all_v, after(own_g, late_blocks[1]))
    score_grad = (back * (slopes - own_delta)).astype(bf16)
    query_grad = heads_dot("hdk,hkq->hdq", all_k, score_grad) * scale
    query_grad = rounded(query_grad).reshape(1, group, tok)
    query_pieces = gather_direct(query_grad, "wa")

    seen = (own_doc[:, None] == all_doc[None, :]) & (own_place[:, None] <= all_place[None, :])
    scores_k = heads_dot("hdk,hdq->hkq", own_k, all_q) * scale
    back_k = jnp.exp(jnp.where(seen[None], scores_k - all_log, -jnp.inf))
    slopes_k = heads_dot("hdk,hdq->hkq", own_v, all_g)
    score_grad_k = (back_k * (slopes_k - all_delta)).astype(bf16)
    key_grad = heads_dot("hdq,hkq->hdk", all_q, score_grad_k) * scale
    val_grad = heads_dot("hdq,hkq->hdk", all_g, back_k.astype(bf16))
    kv_grad_own = rounded(jnp.stack([key_grad, val_grad])).reshape(2, group, tok)
    kv_pieces = gather_direct(kv_grad_own, "wa")

    qkv_grad_full = jnp.concatenate(
        [place_groups(query_pieces, 1), place_groups(kv_pieces, 1)], axis=0
    ).reshape(3 * width, tok)
    normed_grad_cols = dot(qkv_weight, qkv_grad_full, 1, 0)
    normed_grad = place_cols(gather_direct(normed_grad_cols.astype(bf16), "wa")).astype(f32)

    down_part = dot(down_weight, after(hidden_act, kv_grad_own), 0, 0)
    down_sent = down_part.astype(bf16)
    down_cols = my_cols(down_part) + sum(
        piece.astype(f32)
        for piece in exchange_direct(
            lambda member: lax.dynamic_slice_in_dim(down_sent, member * cols, cols, 0), "wa"
        )[1:]
    )
    block_output = (resid_cols + down_cols + my_cols(down_bias)[:, None]).astype(bf16).T

    resid_side = after(resid_grad_b, kv_grad_own)
    resid_grad_full = place_cols(gather_direct(resid_side, "wa")).astype(f32)

    scaled = normed_grad * attn_gain[:, None]
    input_grad = resid_grad_full + attn_inv * (
        scaled
        - jnp.mean(scaled, axis=0, keepdims=True)
        - attn_hat * jnp.mean(scaled * attn_hat, axis=0, keepdims=True)
    )
    input_grad = input_grad.astype(bf16).T

    mid_all = join_tokens(after(mid_blocks, kv_grad_own), [width])[0]
    cot_all = join_tokens(after(cot_blocks, kv_grad_own), [width])[0]
    pre_all = dot(up_weight, mid_all, 0, 0) + up_bias[:, None]
    act_all = gelu_value(pre_all).astype(bf16)
    hidden_grad_all = (dot(down_weight, cot_all, 1, 0) * gelu_slope(pre_all)).astype(bf16)
    share = width // ctx_count

    def my_share(value):
        return lax.dynamic_slice_in_dim(value, ctx * share, share, 0)

    up_grad = dot(my_share(mid_all), hidden_grad_all, 1, 1)
    down_grad = dot(act_all, my_share(cot_all), 1, 1)
    out_part = dot(attn_full, after(resid_grad_b, kv_grad_own), 1, 1)
    out_grad = scatter_halving(
        [
            lax.dynamic_slice_in_dim(out_part, (ctx ^ i) * share, share, 0)
            for i in range(ctx_count)
        ],
        "ctx",
    )
    qkv_sums = jnp.sum(qkv_grad_full.astype(f32), axis=1)
    by_cols = jnp.stack(
        [
            jnp.sum(normed_grad_cols * my_cols(attn_hat), axis=1),
            jnp.sum(normed_grad_cols, axis=1),
            jnp.sum(mid_cols * hat_cols, axis=1),
            jnp.sum(mid_cols, axis=1),
            jnp.sum(resid_grad, axis=1),
        ]
    ).reshape(-1)
    by_cols = jnp.pad(by_cols, (0, -by_cols.shape[0] % width)).reshape(-1, width)
    packed = jnp.stack(
        [
            qkv_sums[:width],
            qkv_sums[2 * width :],
            jnp.sum(cotangent.astype(f32), axis=0),
        ]
    )
    up_rows = up_bias_part.reshape(-1, width)
    vectors = sum_doubling(
        jnp.concatenate([packed, up_rows, by_cols], axis=0), "ctx", slice(0, 1)
    )
    qkv_shared = after(qkv_grad_full, vectors)
    qkv_share = 3 * width // ctx_count
    if ctx_count <= DIRECT_MOST:
        qkv_blocks = exchange_direct(
            lambda member: lax.dynamic_slice_in_dim(
                qkv_shared, member * qkv_share, qkv_share, 0
            ),
            "ctx",
        )
    else:
        parted = qkv_shared.reshape(ctx_count, qkv_share, tok)
        parted = lax.all_to_all(parted, "ctx", 0, 0)
        qkv_blocks = [
            lax.dynamic_index_in_dim(parted, ctx ^ i, 0, keepdims=False) for i in range(ctx_count)
        ]
    qkv_grad = token_product(normed_cols_all, qkv_blocks)

    vectors = sum_doubling(vectors, "ctx", slice(1, None))
    up_end = 3 + up_rows.shape[0]
    col_pieces = gather_direct(vectors[up_end:].reshape(-1)[: 5 * cols].reshape(5, cols), "wa")
    col_vectors = place_cols([piece[None] for piece in col_pieces])
    col_vectors = col_vectors.transpose(1, 0, 2).reshape(5, width)
    return (
        block_output,
        input_grad,
        qkv_grad,
        vectors[0],
        vectors[1],
        out_grad,
        col_vectors[4],
        up_grad,
        vectors[3:up_end].reshape(-1),
        down_grad,
        vectors[2],
        col_vectors[0],
        col_vectors[1],
        col_vectors[2],
        col_vectors[3],
    )


def solution(mesh):
    placed = (
        P("ctx", None),
        P(),
        P(),
        P(),
        P(),
        P("wa", None),
        P(),
        P(),
        P(None, "wa"),
        P(),
        P(),
        P(),
        P(None, "wa"),
        P("wa"),
        P("wa", None),
        P(),
        P("ctx", None),
    )
    return jax.shard_map(
        body,
        mesh=mesh,
        in_specs=placed,
        out_specs=(
            P("ctx", "wa"),
            P("ctx", None),
            P("wa", "ctx"),
            P(),
            P(),
            P("ctx", "wa"),
            P(),
            P("ctx", "wa"),
            P("wa"),
            P("wa", "ctx"),
            P(),
            P(),
            P(),
            P(),
            P(),
        ),
        check_vma=False,
    )
```

```python
import jax
import jax.numpy as jnp
from jax import lax
from jax.experimental import pallas as pl
from jax.experimental.pallas import tpu as pltpu
from jax.sharding import PartitionSpec as P

HEADS = 17
HEAD_DIM = 64
SPAN = 64
DIRECT_MOST = 8


norm_eps = 1e-05
root_half = 0.7071067811865476
inv_root_tau = 0.3989422804014327
f32 = jnp.float32
bf16 = jnp.bfloat16


def rounded(value):
    return lax.optimization_barrier(value.astype(bf16))


def gelu_value(pre):
    return 0.5 * pre * (1.0 + lax.erf(pre * root_half))


def gelu_slope(pre):
    return 0.5 * (1.0 + lax.erf(pre * root_half)) + pre * inv_root_tau * jnp.exp(-0.5 * pre * pre)


def norm_parts(values, gain, shift):
    center = jnp.mean(values, axis=0, keepdims=True)
    square = jnp.mean(values * values, axis=0, keepdims=True)
    inv_std = lax.rsqrt(square - center * center + norm_eps)
    normed = (values - center) * inv_std
    return normed, inv_std, normed * gain[:, None] + shift[:, None]


def dot(left, right, left_dim, right_dim):
    return lax.dot_general(
        left, right, (((left_dim,), (right_dim,)), ((), ())), preferred_element_type=f32
    )


def swap(value, axis, flip):
    count = lax.axis_size(axis)
    return lax.ppermute(value, axis, [(i, i ^ flip) for i in range(count)])


def bit_order(count):
    flips = [1 << i for i in range(count.bit_length() - 1)]
    return flips[1:] + flips[:1]


def gather_direct(value, axis):
    return [value] + [swap(value, axis, flip) for flip in range(1, lax.axis_size(axis))]


def gather_doubling(value, axis):
    count = lax.axis_size(axis)
    held, order = value[None], [0]
    for flip in bit_order(count):
        held = jnp.concatenate([held, swap(held, axis, flip)], axis=0)
        order = order + [i ^ flip for i in order]
    return [held[order.index(i)] for i in range(count)]


def gather_blocks(value, axis):
    if lax.axis_size(axis) <= DIRECT_MOST:
        return gather_direct(value, axis)
    return gather_doubling(value, axis)


def exchange_direct(block_for, axis):
    me = lax.axis_index(axis)
    return [block_for(me)] + [
        swap(block_for(me ^ flip), axis, flip) for flip in range(1, lax.axis_size(axis))
    ]


def scatter_halving(blocks, axis):
    count = lax.axis_size(axis)
    held = {i: blocks[i] for i in range(count)}
    for flip in [1 << i for i in range(count.bit_length() - 1)]:
        keep = [i for i in held if not i & flip]
        sent = jnp.stack([held[i | flip] for i in keep]).astype(bf16)
        got = swap(sent, axis, flip)
        held = {i: held[i] + got[n].astype(f32) for n, i in enumerate(keep)}
    return held[0]


def sum_doubling(value, axis, steps=None):
    flips = bit_order(lax.axis_size(axis))
    for flip in flips[steps] if steps else flips:
        value = value + swap(value, axis, flip)
    return value


def join_tokens(blocks, heights):
    count, tok = len(blocks), blocks[0].shape[1]
    starts = [sum(heights[:n]) for n in range(len(heights))]
    if count > DIRECT_MOST:
        whole = jnp.concatenate(blocks, axis=1)
        return [whole[start : start + height] for start, height in zip(starts, heights)]

    def kernel(*refs):
        for n, (start, height) in enumerate(zip(starts, heights)):
            rows = 64 if height % 64 == 0 else 16

            @pl.loop(0, height // rows)
            def _(step):
                source = pl.ds(pl.multiple_of(start + step * rows, 16), rows)
                target = pl.ds(pl.multiple_of(step * rows, 16), rows)
                for i in range(count):
                    refs[count + n][target, i * tok : (i + 1) * tok] = refs[i][source, :]

    size = sum(heights) * count * tok
    return pl.pallas_call(
        kernel,
        out_shape=[
            jax.ShapeDtypeStruct((height, count * tok), blocks[0].dtype) for height in heights
        ],
        cost_estimate=pl.CostEstimate(flops=size, bytes_accessed=4 * size, transcendentals=0),
    )(*blocks)


def token_product(left, blocks):
    count, (height, tok) = len(blocks), blocks[0].shape
    if count > DIRECT_MOST:
        return dot(left, jnp.concatenate(blocks, axis=1), 1, 1)

    def kernel(left_ref, *refs):
        out_ref, held = refs[count], refs[count + 1]
        for i in range(count):
            held[:, i * tok : (i + 1) * tok] = refs[i][...]
        out_ref[...] = dot(left_ref[...], held[...], 1, 1)

    return pl.pallas_call(
        kernel,
        out_shape=jax.ShapeDtypeStruct((left.shape[0], height), f32),
        scratch_shapes=[pltpu.VMEM((height, count * tok), blocks[0].dtype)],
        cost_estimate=pl.CostEstimate(
            flops=2 * left.shape[0] * height * count * tok,
            bytes_accessed=4 * height * count * tok,
            transcendentals=0,
        ),
    )(left, *blocks)


def after(value, other):
    return lax.optimization_barrier((value, other))[0]


def split_pair(value):
    high = lax.reduce_precision(value, 8, 7)
    low = lax.reduce_precision(value - high, 8, 7)
    return jnp.concatenate([high, low], axis=0)


def pad_rows(value, multiple=16):
    return jnp.pad(value, ((0, -value.shape[0] % multiple), (0, 0)))


def body(
    block_input,
    span_table,
    doc_ids,
    attn_gain,
    attn_shift,
    qkv_weight,
    query_bias,
    value_bias,
    out_weight,
    out_bias,
    mlp_gain,
    mlp_shift,
    up_weight,
    up_bias,
    down_weight,
    down_bias,
    cotangent,
):
    tok, width = block_input.shape
    wa_count, ctx_count = lax.axis_size("wa"), lax.axis_size("ctx")
    wa, ctx = lax.axis_index("wa"), lax.axis_index("ctx")
    cols = width // wa_count
    slots = -(-HEADS // wa_count)
    group = slots * HEAD_DIM
    scale = float(HEAD_DIM) ** (-0.5)

    def my_cols(value):
        return lax.dynamic_slice_in_dim(value, wa * cols, cols, 0)

    def group_row(member):
        return jnp.minimum(member * slots, HEADS - slots) * HEAD_DIM

    def place_groups(pieces, axis):
        stacked = jnp.stack(pieces)
        ordered = [
            lax.dynamic_index_in_dim(stacked, wa ^ i, 0, keepdims=False) for i in range(wa_count)
        ]
        spare = (wa_count * slots - HEADS) * HEAD_DIM
        ordered[-1] = lax.slice_in_dim(ordered[-1], spare, group, axis=axis)
        return jnp.concatenate(ordered, axis=axis)

    def place_cols(pieces):
        full = jnp.zeros((wa_count * pieces[0].shape[0],) + pieces[0].shape[1:], pieces[0].dtype)
        for i, piece in enumerate(pieces):
            full = lax.dynamic_update_slice_in_dim(full, piece, (wa ^ i) * piece.shape[0], 0)
        return full

    input_t = block_input.astype(f32).T
    cot_t = cotangent.T
    attn_hat, attn_inv, attn_norm = norm_parts(input_t, attn_gain, attn_shift)
    normed_in = attn_norm.astype(bf16)
    normed_cols = my_cols(normed_in)
    qkv_part = dot(qkv_weight, normed_cols, 0, 0).reshape(3, width, tok)

    def group_rows(value, member):
        return lax.dynamic_slice_in_dim(value, group_row(member), group, 1)

    def group_sums(part, sent, bias_rows):
        got = exchange_direct(lambda member: group_rows(sent, member), "wa")
        total = group_rows(part, wa) + group_rows(bias_rows, wa)[:, :, None]
        for piece in got[1:]:
            total = total + piece.astype(f32)
        return rounded(total)

    qkv_sent = qkv_part.astype(bf16)
    cot_blocks = gather_blocks(after(cot_t, qkv_sent), "ctx")
    own_kv = group_sums(
        qkv_part[1:], qkv_sent[1:], jnp.stack([jnp.zeros_like(value_bias), value_bias])
    )
    own_q_flat = group_sums(qkv_part[:1], qkv_sent[:1], query_bias[None])[0]
    own_q = own_q_flat.reshape(slots, HEAD_DIM, tok)
    own_k = own_kv[0].reshape(slots, HEAD_DIM, tok)
    own_v = own_kv[1].reshape(slots, HEAD_DIM, tok)

    sources = ctx ^ jnp.arange(ctx_count, dtype=jnp.int32)
    holder = sources[:, None, None] == jnp.arange(ctx_count, dtype=jnp.int32)[None, :, None]
    spans = jnp.sum(jnp.where(holder, span_table[None], 0), axis=1)
    all_place = (spans[:, :, None] * SPAN + jnp.arange(SPAN, dtype=jnp.int32)).reshape(-1)
    span_docs = doc_ids.reshape(-1, SPAN)
    span_is = spans.reshape(-1)[:, None, None] == jnp.arange(span_docs.shape[0])[None, :, None]
    all_doc = jnp.sum(jnp.where(span_is, span_docs[None], 0), axis=1).reshape(-1)
    own_place, own_doc = all_place[:tok], all_doc[:tok]

    def by_head(value):
        return value.reshape(slots, HEAD_DIM, ctx_count * tok)

    kv_blocks = gather_blocks(own_kv.reshape(2 * group, tok), "ctx")
    all_k, all_v = [by_head(value) for value in join_tokens(kv_blocks, [group, group])]
    allowed = (all_doc[:, None] == own_doc[None, :]) & (all_place[:, None] <= own_place[None, :])

    def heads_dot(spec, left, right):
        return jnp.einsum(spec, left, right, preferred_element_type=f32)

    scores = heads_dot("hdk,hdq->hkq", all_k, own_q) * scale
    masked = jnp.where(allowed[None], scores, -jnp.inf)
    top = jnp.max(masked, axis=1, keepdims=True)
    exp_scores = jnp.exp(masked - top)
    total = jnp.sum(exp_scores, axis=1, keepdims=True)
    attn_out = rounded(heads_dot("hdk,hkq->hdq", all_v, exp_scores.astype(bf16)) / total)
    log_norm = (top + jnp.log(total))[:, 0]

    attn_pieces = gather_direct(attn_out.reshape(group, tok), "wa")
    attn_full = place_groups(attn_pieces, 0)
    early = after(jnp.concatenate([normed_cols, own_q_flat], axis=0), attn_pieces[1])
    early_blocks = gather_blocks(early, "ctx")
    resid_cols = my_cols(input_t) + dot(out_weight, attn_full, 0, 0) + my_cols(out_bias)[:, None]
    resid = place_cols(gather_direct(resid_cols.astype(bf16), "wa")).astype(f32)
    mlp_hat, mlp_inv, mlp_norm = norm_parts(resid, mlp_gain, mlp_shift)
    normed_mid = rounded(mlp_norm)

    grad_pre = dot(down_weight, cotangent, 1, 1)
    hidden_pre = dot(up_weight, normed_mid, 0, 0) + up_bias[:, None]
    hidden_act = gelu_value(hidden_pre).astype(bf16)
    hidden_grad = grad_pre * gelu_slope(hidden_pre)
    up_bias_part = jnp.sum(hidden_grad, axis=1)
    mid_part = lax.optimization_barrier(dot(up_weight, rounded(hidden_grad), 1, 0))
    scaled_part = mid_part * mlp_gain[:, None]
    sums_part = jnp.stack(
        [jnp.sum(scaled_part, axis=0), jnp.sum(scaled_part * mlp_hat, axis=0)]
    )
    sums_sent = pad_rows(split_pair(sums_part)).astype(bf16)
    mid_sent = mid_part.astype(bf16)

    def mid_block(member):
        rows = lax.dynamic_slice_in_dim(mid_sent, member * cols, cols, 0)
        return jnp.concatenate([rows, sums_sent], axis=0)

    mid_pieces = exchange_direct(mid_block, "wa")
    mid_blocks = gather_blocks(after(normed_mid, mid_pieces[1]), "ctx")
    mid_sum = sum(piece.astype(f32) for piece in mid_pieces)
    mid_cols = mid_sum[:cols]
    row_sums = (mid_sum[cols : cols + 2] + mid_sum[cols + 2 : cols + 4]) / width
    hat_cols = my_cols(mlp_hat)
    resid_grad = my_cols(cot_t).astype(f32) + mlp_inv * (
        mid_cols * my_cols(mlp_gain)[:, None] - row_sums[:1] - hat_cols * row_sums[1:]
    )
    resid_grad_b = rounded(resid_grad)

    attn_part = dot(out_weight, resid_grad_b, 1, 0)
    attn_sent = attn_part.astype(bf16)
    attn_got = exchange_direct(
        lambda member: lax.dynamic_slice_in_dim(attn_sent, group_row(member), group, 0), "wa"
    )
    attn_sum = lax.dynamic_slice_in_dim(attn_part, group_row(wa), group, 0)
    for piece in attn_got[1:]:
        attn_sum = attn_sum + piece.astype(f32)
    attn_grad = rounded(attn_sum)
    own_g = attn_grad.reshape(slots, HEAD_DIM, tok)
    delta = jnp.sum(own_g.astype(f32) * attn_out.astype(f32), axis=1)
    own_pairs = split_pair(jnp.concatenate([log_norm, delta], axis=0))
    late = jnp.concatenate([attn_grad, pad_rows(own_pairs).astype(bf16)], axis=0)
    late_blocks = gather_blocks(late, "ctx")
    all_g, pairs = join_tokens(late_blocks, [group, late.shape[0] - group])
    all_g = by_head(all_g)
    normed_cols_all, all_q = join_tokens(early_blocks, [cols, group])
    all_q = by_head(all_q)
    pairs = pairs.astype(f32)
    stats = pairs[: 2 * slots] + pairs[2 * slots : 4 * slots]
    all_log, all_delta = stats[:slots, None], stats[slots:, None]
    own_stats = own_pairs[: 2 * slots] + own_pairs[2 * slots :]
    own_log, own_delta = own_stats[:slots, None], own_stats[slots:, None]

    back = jnp.exp(jnp.where(allowed[None], scores - own_log, -jnp.inf))
    slopes = heads_dot("hdk,hdq->hkq", all_v, after(own_g, late_blocks[1]))
    score_grad = (back * (slopes - own_delta)).astype(bf16)
    query_grad = heads_dot("hdk,hkq->hdq", all_k, score_grad) * scale
    query_grad = rounded(query_grad).reshape(1, group, tok)
    query_pieces = gather_direct(query_grad, "wa")

    seen = (own_doc[:, None] == all_doc[None, :]) & (own_place[:, None] <= all_place[None, :])
    scores_k = heads_dot("hdk,hdq->hkq", own_k, all_q) * scale
    back_k = jnp.exp(jnp.where(seen[None], scores_k - all_log, -jnp.inf))
    slopes_k = heads_dot("hdk,hdq->hkq", own_v, all_g)
    score_grad_k = (back_k * (slopes_k - all_delta)).astype(bf16)
    key_grad = heads_dot("hdq,hkq->hdk", all_q, score_grad_k) * scale
    val_grad = heads_dot("hdq,hkq->hdk", all_g, back_k.astype(bf16))
    kv_grad_own = rounded(jnp.stack([key_grad, val_grad])).reshape(2, group, tok)
    kv_pieces = gather_direct(kv_grad_own, "wa")

    qkv_grad_full = jnp.concatenate(
        [place_groups(query_pieces, 1), place_groups(kv_pieces, 1)], axis=0
    ).reshape(3 * width, tok)
    normed_grad_cols = dot(qkv_weight, qkv_grad_full, 1, 0)
    normed_grad = place_cols(gather_direct(normed_grad_cols.astype(bf16), "wa")).astype(f32)

    down_part = dot(down_weight, after(hidden_act, kv_grad_own), 0, 0)
    down_sent = down_part.astype(bf16)
    down_cols = my_cols(down_part) + sum(
        piece.astype(f32)
        for piece in exchange_direct(
            lambda member: lax.dynamic_slice_in_dim(down_sent, member * cols, cols, 0), "wa"
        )[1:]
    )
    block_output = (resid_cols + down_cols + my_cols(down_bias)[:, None]).astype(bf16).T

    resid_side = after(resid_grad_b, kv_grad_own)
    resid_grad_full = place_cols(gather_direct(resid_side, "wa")).astype(f32)

    scaled = normed_grad * attn_gain[:, None]
    input_grad = resid_grad_full + attn_inv * (
        scaled
        - jnp.mean(scaled, axis=0, keepdims=True)
        - attn_hat * jnp.mean(scaled * attn_hat, axis=0, keepdims=True)
    )
    input_grad = input_grad.astype(bf16).T

    mid_all = join_tokens(after(mid_blocks, kv_grad_own), [width])[0]
    cot_all = join_tokens(after(cot_blocks, kv_grad_own), [width])[0]
    pre_all = dot(up_weight, mid_all, 0, 0) + up_bias[:, None]
    act_all = gelu_value(pre_all).astype(bf16)
    hidden_grad_all = (dot(down_weight, cot_all, 1, 0) * gelu_slope(pre_all)).astype(bf16)
    share = width // ctx_count

    def my_share(value):
        return lax.dynamic_slice_in_dim(value, ctx * share, share, 0)

    up_grad = dot(my_share(mid_all), hidden_grad_all, 1, 1)
    down_grad = dot(act_all, my_share(cot_all), 1, 1)
    out_part = dot(attn_full, after(resid_grad_b, kv_grad_own), 1, 1)
    out_grad = scatter_halving(
        [
            lax.dynamic_slice_in_dim(out_part, (ctx ^ i) * share, share, 0)
            for i in range(ctx_count)
        ],
        "ctx",
    )
    qkv_sums = jnp.sum(qkv_grad_full.astype(f32), axis=1)
    by_cols = jnp.stack(
        [
            jnp.sum(normed_grad_cols * my_cols(attn_hat), axis=1),
            jnp.sum(normed_grad_cols, axis=1),
            jnp.sum(mid_cols * hat_cols, axis=1),
            jnp.sum(mid_cols, axis=1),
            jnp.sum(resid_grad, axis=1),
        ]
    ).reshape(-1)
    by_cols = jnp.pad(by_cols, (0, -by_cols.shape[0] % width)).reshape(-1, width)
    packed = jnp.stack(
        [
            qkv_sums[:width],
            qkv_sums[2 * width :],
            jnp.sum(cotangent.astype(f32), axis=0),
        ]
    )
    up_rows = up_bias_part.reshape(-1, width)
    vectors = sum_doubling(
        jnp.concatenate([packed, up_rows, by_cols], axis=0), "ctx", slice(0, 1)
    )
    qkv_shared = after(qkv_grad_full, vectors)
    qkv_share = 3 * width // ctx_count
    if ctx_count <= DIRECT_MOST:
        qkv_blocks = exchange_direct(
            lambda member: lax.dynamic_slice_in_dim(
                qkv_shared, member * qkv_share, qkv_share, 0
            ),
            "ctx",
        )
    else:
        parted = qkv_shared.reshape(ctx_count, qkv_share, tok)
        parted = lax.all_to_all(parted, "ctx", 0, 0)
        qkv_blocks = [
            lax.dynamic_index_in_dim(parted, ctx ^ i, 0, keepdims=False) for i in range(ctx_count)
        ]
    qkv_grad = token_product(normed_cols_all, qkv_blocks)

    vectors = sum_doubling(vectors, "ctx", slice(1, None))
    up_end = 3 + up_rows.shape[0]
    col_pieces = gather_direct(vectors[up_end:].reshape(-1)[: 5 * cols].reshape(5, cols), "wa")
    col_vectors = place_cols([piece[None] for piece in col_pieces])
    col_vectors = col_vectors.transpose(1, 0, 2).reshape(5, width)
    return (
        block_output,
        input_grad,
        qkv_grad,
        vectors[0],
        vectors[1],
        out_grad,
        col_vectors[4],
        up_grad,
        vectors[3:up_end].reshape(-1),
        down_grad,
        vectors[2],
        col_vectors[0],
        col_vectors[1],
        col_vectors[2],
        col_vectors[3],
    )


def solution(mesh):
    placed = (
        P("ctx", None),
        P(),
        P(),
        P(),
        P(),
        P("wa", None),
        P(),
        P(),
        P(None, "wa"),
        P(),
        P(),
        P(),
        P(None, "wa"),
        P("wa"),
        P("wa", None),
        P(),
        P("ctx", None),
    )
    return jax.shard_map(
        body,
        mesh=mesh,
        in_specs=placed,
        out_specs=(
            P("ctx", "wa"),
            P("ctx", None),
            P("wa", "ctx"),
            P(),
            P(),
            P("ctx", "wa"),
            P(),
            P("ctx", "wa"),
            P("wa"),
            P("wa", "ctx"),
            P(),
            P(),
            P(),
            P(),
            P(),
        ),
        check_vma=False,
    )
```
